256 devices in a mesh: row: 16 (over x_lo, z), col: 4 (over x_hi, core), slab: 4 (over y).
Axes of the slice: x: 4 (x_hi: 2, x_lo: 2; x = x_hi * 2 + x_lo), y: 4, z: 8, core: 2. Of those that a mesh axis runs over, the one named last changes fastest.
Arguments:
- inputs: bfloat16 [32, 64, 6144], P('col', None, ('row', 'slab')), may hold values from -6 to 6
- first_weight: bfloat16 [3, 3, 6144, 6144], P(None, None, ('row', 'slab'), 'col'), may hold values from -0.02734375 to 0.02734375
- second_weight: bfloat16 [3, 3, 6144, 6144], P(None, None, 'col', ('row', 'slab')), may hold values from -0.02734375 to 0.02734375
Outputs:
- result: bfloat16 [32, 64, 6144], P('col', None, ('row', 'slab'))
The draws below stay inside these ranges and needn't reach their ends.
All inputs are finite; a program needn't handle non-finite values.
Results may differ from the reference program's by a relative error of at most 0.015.
Values may be sent and summed in bfloat16 or wider, within the bound.
No kernel may reach another device: no remote copies, remote signals or barrier semaphores. Data moves between devices by JAX's collectives and lax.ppermute only.
A program may use at most 128 MiB of HBM per device.

```python
import jax
import jax.numpy as jnp
from jax import lax

C = 6144
H = 32
W = 64


def level_of(stream_key, dims, shards, smallest, high):
    def one(position, shards_of):
        steps = jax.random.uniform(jax.random.fold_in(jax.random.fold_in(stream_key, 6), position), (shards_of,), jnp.float32, smallest / len(shards), high / len(shards))
        return jnp.repeat(jnp.exp(steps), dims[position] // shards_of).reshape((-1,) + (1,) * (len(dims) - position - 1))

    loudness = one(*shards[0])
    for cut in shards[1:]:
        loudness = loudness * one(*cut)
    return loudness


def bell_draw(own_key, shape, spread, most, cuts=(), dtype=jnp.bfloat16):
    drawn = spread * jax.random.normal(own_key, shape, jnp.float32)
    if cuts:
        drawn = drawn * level_of(own_key, shape, cuts, -0.22, 0.18)
    return jnp.clip(drawn, -most, most).astype(dtype)


def setup_inputs(seed: int = 0) -> dict:
    arg_keys = jax.random.split(jax.random.key(seed), 4)
    return {
        "inputs": bell_draw(arg_keys[0], (H, W, C), 1.0, 6.0, ((0, 4), (2, 64))),
        "first_weight": bell_draw(arg_keys[1], (3, 3, C, C), (9 * C) ** -0.5, 0.02734375, ((2, 64), (3, 4))),
        "second_weight": bell_draw(arg_keys[2], (3, 3, C, C), (9 * C) ** -0.5, 0.02734375, ((2, 4), (3, 64))),
    }


def convolve(image, kernel):
    output = lax.conv_general_dilated(image[None].astype(jnp.float32), kernel.astype(jnp.float32), (1, 1), ((1, 1), (1, 1)), dimension_numbers=("NHWC", "HWIO", "NHWC"), precision=lax.Precision.HIGHEST)
    return output[0]


def reference(inputs, first_weight, second_weight):
    first = convolve(inputs, first_weight)
    hidden = jax.nn.silu(first).astype(jnp.bfloat16)
    second = convolve(hidden, second_weight)
    return (inputs.astype(jnp.float32) + second).astype(jnp.bfloat16)
```

```python
import functools

import jax
import jax.numpy as jnp
from jax import lax
from jax.experimental import pallas as pl
from jax.experimental.pallas import tpu as pltpu
from jax.sharding import Mesh, PartitionSpec as P

AXES = ("xl", "z", "xh", "core", "y")
H, W, B = 32, 64, 384
barrier = lax.optimization_barrier


def shift(name, by):
    n = lax.axis_size(name)
    return [(i, (i + by) % n) for i in range(n)]


def fill_taps(x_at, taps):
    zero = jnp.zeros((W, 3 * B), jnp.bfloat16)
    taps[:W, :] = zero
    taps[(H + 1) * W :, :] = zero
    step = 4 * W
    column = lax.broadcasted_iota(jnp.int32, (step, B), 0) % W
    for k in range(H * W // step):
        x = x_at(k * step, step)
        wide = x.astype(jnp.float32)
        rows = slice(W + k * step, W + (k + 1) * step)
        left = jnp.where(column == 0, 0.0, pltpu.roll(wide, 1, 0))
        right = jnp.where(column == W - 1, 0.0, pltpu.roll(wide, step - 1, 0))
        taps[rows, :B] = left.astype(jnp.bfloat16)
        taps[rows, B : 2 * B] = x
        taps[rows, 2 * B :] = right.astype(jnp.bfloat16)


def first_kernel(y_ref, x_ref, own, p1, p2, p3, out_ref, taps, kernel, sems):
    y = y_ref[0]
    copies = [
        pltpu.make_async_copy(
            own.at[:, :, pl.ds(pl.multiple_of(y * B, B), B)], kernel.at[:, pl.ds(0, 96), :], sems.at[0]
        )
    ]
    for s, piece in enumerate((p1, p2, p3), 1):
        copies.append(
            pltpu.make_async_copy(piece, kernel.at[:, pl.ds(s * 96, 96), :], sems.at[s])
        )
    for copy in copies:
        copy.start()
    fill_taps(lambda at, n: x_ref[at : at + n, :], taps)
    for copy in copies:
        copy.wait()
    step = 512
    for k in range(H * W // step):
        total = None
        for v in range(3):
            part = jnp.dot(
                taps[k * step + v * W : k * step + v * W + step, :],
                kernel[3 * v : 3 * v + 3].reshape(3 * B, B),
                preferred_element_type=jnp.float32,
            )
            total = part if total is None else total + part
        out_ref[k * step : (k + 1) * step, :] = total.astype(jnp.bfloat16)


def second_kernel(n_pieces, ids_ref, own, p1, p2, p3, *refs):
    pieces = refs[:n_pieces]
    out_ref, hidden, taps, kernel, sems = refs[n_pieces:]
    y = ids_ref[0]
    copies = []
    for i, piece in enumerate(pieces):
        at = pl.multiple_of(ids_ref[1 + i] * 128, 128)
        copies.append(pltpu.make_async_copy(piece, hidden.at[pl.ds(at, 128), :], sems.at[i]))
    copies.append(
        pltpu.make_async_copy(
            own.at[:, :, pl.ds(pl.multiple_of(y * B, B), B)],
            kernel.at[:, pl.ds(0, 96), :],
            sems.at[n_pieces],
        )
    )
    for s, piece in enumerate((p1, p2, p3), 1):
        copies.append(
            pltpu.make_async_copy(piece, kernel.at[:, pl.ds(s * 96, 96), :], sems.at[n_pieces + s])
        )
    for copy in copies:
        copy.start()
    for copy in copies:
        copy.wait()
    fill_taps(lambda at, n: hidden[at : at + n, :], taps)
    step = 512
    for k in range(H * W // step):
        total = None
        for v in range(3):
            for b in range(3):
                part = lax.dot_general(
                    taps[k * step + v * W : k * step + v * W + step, b * B : (b + 1) * B],
                    kernel[3 * v + b],
                    (((1,), (1,)), ((), ())),
                    preferred_element_type=jnp.float32,
                )
                total = part if total is None else total + part
        out_ref[k * step : (k + 1) * step, :] = total.astype(jnp.bfloat16)


ANY = pl.BlockSpec(memory_space=pl.ANY)
SMEM = pl.BlockSpec(memory_space=pltpu.SMEM)
VMEM = pl.BlockSpec(memory_space=pltpu.VMEM)


def first_conv(y, x, own, pieces):
    return pl.pallas_call(
        first_kernel,
        out_shape=jax.ShapeDtypeStruct((H * W, B), jnp.bfloat16),
        in_specs=[SMEM, VMEM, ANY, ANY, ANY, ANY],
        out_specs=VMEM,
        scratch_shapes=[
            pltpu.VMEM(((H + 2) * W, 3 * B), jnp.bfloat16),
            pltpu.VMEM((9, B, B), jnp.bfloat16),
            pltpu.SemaphoreType.DMA((4,)),
        ],
        name="first_conv",
    )(y, x, own, *pieces)


def second_conv(ids, own, weights, pieces):
    n = len(pieces)
    return pl.pallas_call(
        functools.partial(second_kernel, n),
        out_shape=jax.ShapeDtypeStruct((H * W, B), jnp.bfloat16),
        in_specs=[SMEM] + [ANY] * (4 + n),
        out_specs=VMEM,
        scratch_shapes=[
            pltpu.VMEM((H * W, B), jnp.bfloat16),
            pltpu.VMEM(((H + 2) * W, 3 * B), jnp.bfloat16),
            pltpu.VMEM((9, B, B), jnp.bfloat16),
            pltpu.SemaphoreType.DMA((n + 4,)),
        ],
        name="second_conv",
    )(ids, own, *weights, *pieces)


def spread(weight, y):
    out = []
    for s in (1, 3, 2):
        block = lax.dynamic_slice_in_dim(weight, ((y + s) % 4) * B, B, 2)
        out.append(lax.ppermute(block, "y", shift("y", s)))
    return [out[0], out[2], out[1]]


def local(inputs, first_weight, second_weight):
    y = lax.axis_index("y")
    z = lax.axis_index("z")
    xl = lax.axis_index("xl")
    xh = lax.axis_index("xh")
    core = lax.axis_index("core")
    w1 = first_weight.reshape(9, 96, 4 * B)
    w2 = jnp.transpose(second_weight, (0, 1, 3, 2)).reshape(9, 96, 4 * B)

    parts = [inputs] + [lax.ppermute(inputs, "y", shift("y", s)) for s in (1, 2, 3)]
    mine = jnp.concatenate(parts, axis=2)
    x = lax.all_gather(mine, ("xh", "core"), axis=0, tiled=True).reshape(H * W, B)

    k1 = spread(w1, y)
    first = first_conv(y.reshape(1), x, w1, k1)
    w2, *_ = barrier((w2, *k1))
    k2 = spread(w2, y)

    block = H * W // 16
    terms = lax.all_to_all(first.reshape(16, block, B), ("xl", "z"), 0, 0, tiled=True)
    summed = jnp.sum(terms.astype(jnp.float32), axis=0)
    own = jax.nn.silu(summed).astype(jnp.bfloat16)

    other = lax.ppermute(own, "xl", shift("xl", 1))
    pieces, ids = [], [y]
    for start, row in ((own, xl), (other, 1 - xl)):
        pieces.append(start)
        ids.append(row * 8 + z)
        up = down = start
        for k in range(1, 5):
            up = lax.ppermute(up, "z", shift("z", 1))
            pieces.append(up)
            ids.append(row * 8 + (z - k) % 8)
            if k < 4:
                down = lax.ppermute(down, "z", shift("z", -1))
                pieces.append(down)
                ids.append(row * 8 + (z + k) % 8)
    second = second_conv(jnp.stack(ids).astype(jnp.int32), w2, k2, pieces)

    second = second.reshape(2, 2, 512, B)
    keep = lax.dynamic_index_in_dim(second, core, 1, keepdims=False)
    give = lax.dynamic_index_in_dim(second, 1 - core, 1, keepdims=False)
    got = lax.ppermute(give, "core", shift("core", 1))
    both = keep.astype(jnp.float32) + got.astype(jnp.float32)
    half = both.astype(jnp.bfloat16)
    total = both[:, :, :96]
    for s in (1, 2, 3):
        total = total + lax.ppermute(
            half[:, :, s * 96 : (s + 1) * 96], "y", shift("y", -s)
        ).astype(jnp.float32)
    keep = lax.dynamic_index_in_dim(total, xh, 0, keepdims=False)
    give = lax.dynamic_index_in_dim(total, 1 - xh, 0, keepdims=False).astype(jnp.bfloat16)
    got = lax.ppermute(give, "xh", shift("xh", 1))
    result = keep + got.astype(jnp.float32)
    return (inputs.astype(jnp.float32) + result.reshape(inputs.shape)).astype(jnp.bfloat16)


def solution(mesh):
    fine = Mesh(mesh.devices.reshape(2, 8, 2, 2, 4), AXES)
    row_slab, col = ("xl", "z", "y"), ("xh", "core")
    return jax.shard_map(
        local,
        mesh=fine,
        in_specs=(P(col, None, row_slab), P(None, None, row_slab, col), P(None, None, col, row_slab)),
        out_specs=P(col, None, row_slab),
        check_vma=False,
    )
```

```python
import functools

import jax
import jax.numpy as jnp
from jax import lax
from jax.experimental import pallas as pl
from jax.experimental.pallas import tpu as pltpu
from jax.sharding import Mesh, PartitionSpec as P


AXES = ("xl", "z", "xh", "core", "y")
H, W, B = 32, 64, 384


def shift(name, by):
    n = lax.axis_size(name)
    return [(i, (i + by) % n) for i in range(n)]


def fill_taps(x_ref, taps, at, width):
    taps[:W, :] = jnp.zeros((W, 3 * width), jnp.bfloat16)
    taps[(H + 1) * W :, :] = jnp.zeros((W, 3 * width), jnp.bfloat16)
    step = 4 * W
    column = lax.broadcasted_iota(jnp.int32, (step, width), 0) % W

    def body(k, carry):
        start = pl.multiple_of(k * step, step)
        x = x_ref[pl.ds(start, step), at : at + width]
        wide = x.astype(jnp.float32)
        rows = pl.ds(pl.multiple_of(start + W, W), step)
        left = jnp.where(column == 0, 0.0, pltpu.roll(wide, 1, 0))
        right = jnp.where(column == W - 1, 0.0, pltpu.roll(wide, step - 1, 0))
        taps[rows, :width] = left.astype(jnp.bfloat16)
        taps[rows, width : 2 * width] = x
        taps[rows, 2 * width :] = right.astype(jnp.bfloat16)
        return carry

    lax.fori_loop(0, H * W // step, body, 0)


EARLY = 256


def partial_sums(taps, kernel, at, width):
    total = None
    for v in range(3):
        part = jnp.dot(
            taps[pl.ds(pl.multiple_of(at + v * W, W), 512), :],
            kernel[3 * v : 3 * v + 3].reshape(3 * width, B),
            preferred_element_type=jnp.float32,
        )
        total = part if total is None else total + part
    return total


def early_kernel(ids, x0, x1, x2, x3, own, p3, p2, out_ref, late_taps, x_ref, taps, kernel, sems):
    copies = []
    for i, piece in enumerate((x0, x1, x2, x3)):
        rows = pl.ds(pl.multiple_of(ids[1 + i] * 512, 512), 512)
        copies.append(pltpu.make_async_copy(piece, x_ref.at[rows, :], sems.at[i]))
    start = pl.multiple_of(ids[0] * B, 128)
    blocks = (
        (own.at[:, :, pl.ds(start, B)], 0, 96),
        (p3, 96, 96),
        (p2.at[:, pl.ds(0, EARLY - 192), :], 192, EARLY - 192),
    )
    for i, (block, at, size) in enumerate(blocks):
        copies.append(
            pltpu.make_async_copy(block, kernel.at[:, pl.ds(at, size), :], sems.at[4 + i])
        )
    for copy in copies:
        copy.start()
    for copy in copies[:4]:
        copy.wait()
    fill_taps(x_ref, taps, 0, EARLY)
    fill_taps(x_ref, late_taps, EARLY, B - EARLY)
    for copy in copies[4:]:
        copy.wait()

    def body(k, carry):
        at = pl.multiple_of(k * 512, 512)
        out_ref[pl.ds(at, 512), :] = partial_sums(taps, kernel, at, EARLY)
        return carry

    lax.fori_loop(0, 4, body, 0)


def late_kernel(p2, p1, before, taps, out_ref, kernel, sems):
    rest = 288 - EARLY
    copies = [
        pltpu.make_async_copy(
            p2.at[:, pl.ds(EARLY - 192, rest), :], kernel.at[:, pl.ds(0, rest), :], sems.at[0]
        ),
        pltpu.make_async_copy(p1, kernel.at[:, pl.ds(rest, 96), :], sems.at[1]),
    ]
    for copy in copies:
        copy.start()
    for copy in copies:
        copy.wait()

    def body(k, carry):
        at = pl.multiple_of(k * 512, 512)
        total = before[pl.ds(at, 512), :] + partial_sums(taps, kernel, at, B - EARLY)
        out_ref[pl.ds(at, 512), :] = total.astype(jnp.bfloat16)
        return carry

    lax.fori_loop(0, 4, body, 0)


def kernel_copies(ids, at, width, own, pieces, kernel, sems):
    start = pl.multiple_of(ids[0] * B + at, 128)
    copies = []
    for s in range(4):
        for b in range(3):
            if s == 0:
                source = own.at[:, b, :, pl.ds(start, width)]
            else:
                source = pieces[s - 1].at[:, b, :, pl.ds(at, width)]
            rows = pl.ds(pl.multiple_of(lax.rem(ids[0] + 4 - s, 4) * 96, 96), 96)
            target = kernel.at[:, rows, pl.ds(b * width, width)]
            copies.append(pltpu.make_async_copy(source, target, sems.at[3 * s + b]))
    return copies


def dots(taps, kernel, at):
    total = None
    for v in range(3):
        part = lax.dot_general(
            kernel[v],
            taps[pl.ds(pl.multiple_of(at + v * W, W), 512), :],
            (((1,), (1,)), ((), ())),
            preferred_element_type=jnp.float32,
        )
        total = part if total is None else total + part
    return total


def second_kernel(width, n, ids, own, p1, p2, p3, *refs):
    pieces, (keep, give, hidden, taps, kernel, sems, wsems) = refs[:n], refs[n:]
    weights = kernel_copies(ids, 0, width, own, (p1, p2, p3), kernel, wsems)
    copies, count = [], 0
    for piece in pieces:
        for j in range(piece.shape[0]):
            rows = pl.ds(pl.multiple_of(ids[2 + count] * 128, 128), 128)
            copies.append(pltpu.make_async_copy(piece.at[j], hidden.at[rows, :], sems.at[count]))
            count += 1
    for copy in weights + copies:
        copy.start()
    for copy in copies:
        copy.wait()
    fill_taps(hidden, taps, 0, width)
    for copy in weights:
        copy.wait()
    core = ids[1]

    def body(h, carry):
        for ref, c in ((keep, core), (give, 1 - core)):
            at = pl.multiple_of((h * 2 + c) * 512, 512)
            ref[pl.ds(h, 1)] = dots(taps, kernel, at).astype(jnp.bfloat16)[None]
        return carry

    lax.fori_loop(0, 2, body, 0)


ANY = pl.BlockSpec(memory_space=pl.ANY)
SMEM = pl.BlockSpec(memory_space=pltpu.SMEM)
VMEM = pl.BlockSpec(memory_space=pltpu.VMEM)
PARAMS = pltpu.CompilerParams(vmem_limit_bytes=40 << 20)


def early_conv(ids, x, own, p3, p2):
    return pl.pallas_call(
        early_kernel,
        out_shape=(
            jax.ShapeDtypeStruct((H * W, B), jnp.float32),
            jax.ShapeDtypeStruct(((H + 2) * W, 3 * (B - EARLY)), jnp.bfloat16),
        ),
        in_specs=[SMEM] + [ANY] * 7,
        out_specs=(VMEM, VMEM),
        scratch_shapes=[
            pltpu.VMEM((H * W, B), jnp.bfloat16),
            pltpu.VMEM(((H + 2) * W, 3 * EARLY), jnp.bfloat16),
            pltpu.VMEM((9, EARLY, B), jnp.bfloat16),
            pltpu.SemaphoreType.DMA((7,)),
        ],
        compiler_params=PARAMS,
        name="early_conv",
    )(ids, *x, own, p3, p2)


def late_conv(p2, p1, before, taps):
    return pl.pallas_call(
        late_kernel,
        out_shape=jax.ShapeDtypeStruct((H * W, B), jnp.bfloat16),
        in_specs=[ANY, ANY, VMEM, VMEM],
        out_specs=VMEM,
        scratch_shapes=[
            pltpu.VMEM((9, B - EARLY, B), jnp.bfloat16),
            pltpu.SemaphoreType.DMA((2,)),
        ],
        compiler_params=PARAMS,
        name="late_conv",
    )(p2, p1, before, taps)


def second_conv(ids, own, weights, pieces):
    n = len(pieces)
    half = jax.ShapeDtypeStruct((2, B, 512), jnp.bfloat16)
    return pl.pallas_call(
        functools.partial(second_kernel, B, n),
        out_shape=(half, half),
        in_specs=[SMEM] + [ANY] * (4 + n),
        out_specs=(VMEM, VMEM),
        scratch_shapes=[
            pltpu.VMEM((H * W, B), jnp.bfloat16),
            pltpu.VMEM(((H + 2) * W, 3 * B), jnp.bfloat16),
            pltpu.VMEM((3, B, 3 * B), jnp.bfloat16),
            pltpu.SemaphoreType.DMA((16,)),
            pltpu.SemaphoreType.DMA((12,)),
        ],
        compiler_params=PARAMS,
        name="second_conv",
    )(ids, own, *weights, *pieces)


def spread(weight, y, at, width):
    out = []
    for s in (1, 3, 2):
        block = lax.dynamic_slice_in_dim(weight, ((y + s) % 4) * B + at, width, weight.ndim - 1)
        out.append(lax.ppermute(block, "y", shift("y", s)))
    return [out[0], out[2], out[1]]


def layer(inputs, first_weight, second_weight):
    y = lax.axis_index("y")
    z = lax.axis_index("z")
    xl = lax.axis_index("xl")
    xh = lax.axis_index("xh")
    core = lax.axis_index("core")
    w1 = first_weight.reshape(9, 96, 4 * B)
    w2 = jnp.transpose(second_weight, (0, 1, 3, 2))

    parts = [inputs] + [lax.ppermute(inputs, "y", shift("y", s)) for s in (3, 2, 1)]
    mine = jnp.concatenate(parts, axis=2).reshape(512, B)
    far = lax.ppermute(mine, "xh", shift("xh", 1))
    near = lax.ppermute(mine, "core", shift("core", 1))
    both = lax.ppermute(far, "core", shift("core", 1))
    x = (mine, near, far, both)
    cols = [2 * xh + core, 2 * xh + 1 - core, 2 - 2 * xh + core, 3 - 2 * xh - core]
    ids = jnp.stack([y] + cols).astype(jnp.int32)

    k1 = spread(w1, y, 0, B)
    k2 = spread(w2, y, 0, B)

    block = H * W // 16
    before, taps = early_conv(ids, x, w1, k1[2], k1[1])
    first = late_conv(k1[1], k1[0], before, taps)
    terms = lax.all_to_all(first.reshape(16, block, B), ("xl", "z"), 0, 0, tiled=True)
    summed = jnp.sum(terms.astype(jnp.float32), axis=0)
    own = jax.nn.silu(summed).astype(jnp.bfloat16)[None]

    near, far, places = [own], [lax.ppermute(own, "xl", shift("xl", 1))], [[z]]
    up = down = own
    for k in range(1, 5):
        up = lax.ppermute(up, "z", shift("z", 1))
        if k < 4:
            down = lax.ppermute(down, "z", shift("z", -1))
            both, at = jnp.concatenate([up, down]), [(z - k) % 8, (z + k) % 8]
        else:
            both, at = up, [(z - k) % 8]
        near.append(both)
        far.append(lax.ppermute(both, "xl", shift("xl", 1)))
        places.append(at)
    flat = [place for at in places for place in at]
    ids = [y, core] + [xl * 8 + place for place in flat] + [(1 - xl) * 8 + place for place in flat]
    keep, give = second_conv(jnp.stack(ids).astype(jnp.int32), w2, k2, near + far)

    got = lax.ppermute(give, "core", shift("core", 1))
    both = (keep.astype(jnp.float32) + got.astype(jnp.float32)).astype(jnp.bfloat16)
    terms = lax.all_to_all(both.reshape(8, 96, 512), ("xh", "y"), 0, 0, tiled=True)
    total = jnp.sum(terms.astype(jnp.float32), axis=0).T
    return (inputs.astype(jnp.float32) + total.reshape(inputs.shape)).astype(jnp.bfloat16)


def solution(mesh):
    fine = Mesh(mesh.devices.reshape(2, 8, 2, 2, 4), AXES)
    row_slab, col = ("xl", "z", "y"), ("xh", "core")
    return jax.shard_map(
        layer,
        mesh=fine,
        in_specs=(P(col, None, row_slab), P(None, None, row_slab, col), P(None, None, col, row_slab)),
        out_specs=P(col, None, row_slab),
        check_vma=False,
    )
```

```python
import functools

import jax
import jax.numpy as jnp
from jax import lax
from jax.experimental import pallas as pl
from jax.experimental.pallas import tpu as pltpu
from jax.sharding import Mesh, PartitionSpec as P


AXES = ("xl", "z", "xh", "core", "y")
H, W, B = 32, 64, 384


def shift(name, by):
    n = lax.axis_size(name)
    return [(i, (i + by) % n) for i in range(n)]


def fill_taps(x_ref, taps, at, width):
    taps[:W, :] = jnp.zeros((W, 3 * width), jnp.bfloat16)
    taps[(H + 1) * W :, :] = jnp.zeros((W, 3 * width), jnp.bfloat16)
    step = 4 * W
    column = lax.broadcasted_iota(jnp.int32, (step, width), 0) % W

    def body(k, carry):
        start = pl.multiple_of(k * step, step)
        x = x_ref[pl.ds(start, step), at : at + width]
        wide = x.astype(jnp.float32)
        rows = pl.ds(pl.multiple_of(start + W, W), step)
        left = jnp.where(column == 0, 0.0, pltpu.roll(wide, 1, 0))
        right = jnp.where(column == W - 1, 0.0, pltpu.roll(wide, step - 1, 0))
        taps[rows, :width] = left.astype(jnp.bfloat16)
        taps[rows, width : 2 * width] = x
        taps[rows, 2 * width :] = right.astype(jnp.bfloat16)
        return carry

    lax.fori_loop(0, H * W // step, body, 0)


EARLY = 128


def partial_sums(taps, kernel, at, width):
    total = None
    for v in range(3):
        part = jnp.dot(
            taps[pl.ds(pl.multiple_of(at + v * W, W), 512), :],
            kernel[3 * v : 3 * v + 3].reshape(3 * width, B),
            preferred_element_type=jnp.float32,
        )
        total = part if total is None else total + part
    return total


def early_kernel(ids, x0, x1, x2, x3, own, p3, out_ref, late_taps, x_ref, taps, kernel, sems):
    copies = []
    for i, piece in enumerate((x0, x1, x2, x3)):
        rows = pl.ds(pl.multiple_of(ids[1 + i] * 512, 512), 512)
        copies.append(pltpu.make_async_copy(piece, x_ref.at[rows, :], sems.at[i]))
    start = pl.multiple_of(ids[0] * B, 128)
    blocks = (
        (own.at[:, :, pl.ds(start, B)], 0, 96),
        (p3.at[:, pl.ds(0, EARLY - 96), :], 96, EARLY - 96),
    )
    for i, (block, at, size) in enumerate(blocks):
        copies.append(
            pltpu.make_async_copy(block, kernel.at[:, pl.ds(at, size), :], sems.at[4 + i])
        )
    for copy in copies:
        copy.start()
    for copy in copies[:4]:
        copy.wait()
    fill_taps(x_ref, taps, 0, EARLY)
    fill_taps(x_ref, late_taps, EARLY, B - EARLY)
    for copy in copies[4:]:
        copy.wait()

    def body(k, carry):
        at = pl.multiple_of(k * 512, 512)
        out_ref[pl.ds(at, 512), :] = partial_sums(taps, kernel, at, EARLY)
        return carry

    lax.fori_loop(0, 4, body, 0)


def late_kernel(p3, p2, p1, before, taps, out_ref, kernel, sems):
    rest = 192 - EARLY
    blocks = ((p3.at[:, pl.ds(EARLY - 96, rest), :], 0, rest), (p2, rest, 96), (p1, rest + 96, 96))
    copies = []
    for i, (block, at, size) in enumerate(blocks):
        copies.append(pltpu.make_async_copy(block, kernel.at[:, pl.ds(at, size), :], sems.at[i]))
    for copy in copies:
        copy.start()
    for copy in copies:
        copy.wait()

    def body(k, carry):
        at = pl.multiple_of(k * 512, 512)
        total = before[pl.ds(at, 512), :] + partial_sums(taps, kernel, at, B - EARLY)
        out_ref[pl.ds(at, 512), :] = total.astype(jnp.bfloat16)
        return carry

    lax.fori_loop(0, 4, body, 0)


def kernel_copies(ids, at, width, own, pieces, kernel, sems):
    start = pl.multiple_of(ids[0] * B + at, 128)
    copies = []
    for s in range(4):
        for b in range(3):
            if s == 0:
                source = own.at[:, b, :, pl.ds(start, width)]
            else:
                source = pieces[s - 1].at[:, b, :, pl.ds(at, width)]
            rows = pl.ds(pl.multiple_of(lax.rem(ids[0] + 4 - s, 4) * 96, 96), 96)
            target = kernel.at[:, rows, pl.ds(b * width, width)]
            copies.append(pltpu.make_async_copy(source, target, sems.at[3 * s + b]))
    return copies


def dots(taps, kernel, at):
    total = None
    for v in range(3):
        part = lax.dot_general(
            kernel[v],
            taps[pl.ds(pl.multiple_of(at + v * W, W), 512), :],
            (((1,), (1,)), ((), ())),
            preferred_element_type=jnp.float32,
        )
        total = part if total is None else total + part
    return total


def second_kernel(width, n, ids, own, p1, p2, p3, *refs):
    pieces, (keep, give, hidden, taps, kernel, sems, wsems) = refs[:n], refs[n:]
    weights = kernel_copies(ids, 0, width, own, (p1, p2, p3), kernel, wsems)
    copies, count = [], 0
    for piece in pieces:
        for j in range(piece.shape[0]):
            rows = pl.ds(pl.multiple_of(ids[2 + count] * 128, 128), 128)
            copies.append(pltpu.make_async_copy(piece.at[j], hidden.at[rows, :], sems.at[count]))
            count += 1
    for copy in weights + copies:
        copy.start()
    for copy in copies:
        copy.wait()
    fill_taps(hidden, taps, 0, width)
    for copy in weights:
        copy.wait()
    core = ids[1]

    def body(h, carry):
        for ref, c in ((keep, core), (give, 1 - core)):
            at = pl.multiple_of((h * 2 + c) * 512, 512)
            ref[pl.ds(h, 1)] = dots(taps, kernel, at).astype(jnp.bfloat16)[None]
        return carry

    lax.fori_loop(0, 2, body, 0)


ANY = pl.BlockSpec(memory_space=pl.ANY)
SMEM = pl.BlockSpec(memory_space=pltpu.SMEM)
VMEM = pl.BlockSpec(memory_space=pltpu.VMEM)
PARAMS = pltpu.CompilerParams(vmem_limit_bytes=40 << 20)


def early_conv(ids, x, own, p3):
    return pl.pallas_call(
        early_kernel,
        out_shape=(
            jax.ShapeDtypeStruct((H * W, B), jnp.float32),
            jax.ShapeDtypeStruct(((H + 2) * W, 3 * (B - EARLY)), jnp.bfloat16),
        ),
        in_specs=[SMEM] + [ANY] * 6,
        out_specs=(VMEM, VMEM),
        scratch_shapes=[
            pltpu.VMEM((H * W, B), jnp.bfloat16),
            pltpu.VMEM(((H + 2) * W, 3 * EARLY), jnp.bfloat16),
            pltpu.VMEM((9, EARLY, B), jnp.bfloat16),
            pltpu.SemaphoreType.DMA((6,)),
        ],
        compiler_params=PARAMS,
        name="early_conv",
    )(ids, *x, own, p3)


def late_conv(p3, p2, p1, before, taps):
    return pl.pallas_call(
        late_kernel,
        out_shape=jax.ShapeDtypeStruct((H * W, B), jnp.bfloat16),
        in_specs=[ANY, ANY, ANY, VMEM, VMEM],
        out_specs=VMEM,
        scratch_shapes=[
            pltpu.VMEM((9, B - EARLY, B), jnp.bfloat16),
            pltpu.SemaphoreType.DMA((3,)),
        ],
        compiler_params=PARAMS,
        name="late_conv",
    )(p3, p2, p1, before, taps)


def second_conv(ids, own, weights, pieces):
    n = len(pieces)
    half = jax.ShapeDtypeStruct((2, B, 512), jnp.bfloat16)
    return pl.pallas_call(
        functools.partial(second_kernel, B, n),
        out_shape=(half, half),
        in_specs=[SMEM] + [ANY] * (4 + n),
        out_specs=(VMEM, VMEM),
        scratch_shapes=[
            pltpu.VMEM((H * W, B), jnp.bfloat16),
            pltpu.VMEM(((H + 2) * W, 3 * B), jnp.bfloat16),
            pltpu.VMEM((3, B, 3 * B), jnp.bfloat16),
            pltpu.SemaphoreType.DMA((16,)),
            pltpu.SemaphoreType.DMA((12,)),
        ],
        compiler_params=PARAMS,
        name="second_conv",
    )(ids, own, *weights, *pieces)


def spread(weight, y, at, width):
    out = []
    for s in (1, 3, 2):
        block = lax.dynamic_slice_in_dim(weight, ((y + s) % 4) * B + at, width, weight.ndim - 1)
        out.append(lax.ppermute(block, "y", shift("y", s)))
    return [out[0], out[2], out[1]]


def layer(inputs, first_weight, second_weight):
    y = lax.axis_index("y")
    z = lax.axis_index("z")
    xl = lax.axis_index("xl")
    xh = lax.axis_index("xh")
    core = lax.axis_index("core")
    w1 = first_weight.reshape(9, 96, 4 * B)
    w2 = jnp.transpose(second_weight, (0, 1, 3, 2))

    x1, x2, x3 = [lax.ppermute(inputs, "y", shift("y", s)) for s in (1, 2, 3)]
    mine = jnp.concatenate([inputs, x3, x2, x1], axis=2).reshape(512, B)
    far = lax.ppermute(mine, "xh", shift("xh", 1))
    near = lax.ppermute(mine, "core", shift("core", 1))
    both = lax.ppermute(far, "core", shift("core", 1))
    x = (mine, near, far, both)
    cols = [2 * xh + core, 2 * xh + 1 - core, 2 - 2 * xh + core, 3 - 2 * xh - core]
    ids = jnp.stack([y] + cols).astype(jnp.int32)

    k1 = spread(w1, y, 0, B)
    k2 = spread(w2, y, 0, B)

    block = H * W // 16
    before, taps = early_conv(ids, x, w1, k1[2])
    first = late_conv(k1[2], k1[1], k1[0], before, taps)
    terms = lax.all_to_all(first.reshape(16, block, B), ("xl", "z"), 0, 0, tiled=True)
    summed = jnp.sum(terms.astype(jnp.float32), axis=0)
    own = jax.nn.silu(summed).astype(jnp.bfloat16)[None]

    def across(piece):
        return lax.ppermute(piece, "xl", shift("xl", 1))

    def move(piece, by):
        return lax.ppermute(piece, "z", shift("z", by))

    up1, down1, up2, down2 = move(own, 1), move(own, -1), move(own, 2), move(own, -2)
    up3, down3 = move(up1, 2), move(down1, -2)
    up4 = move(up2, 2)
    near = [own, up1, down1, up2, down2, up3, down3, up4]
    far = [across(piece) for piece in near]
    places = [[z], [(z - 1) % 8], [(z + 1) % 8], [(z - 2) % 8], [(z + 2) % 8]]
    places += [[(z - 3) % 8], [(z + 3) % 8], [(z - 4) % 8]]
    flat = [place for at in places for place in at]
    ids = [y, core] + [xl * 8 + place for place in flat] + [(1 - xl) * 8 + place for place in flat]
    keep, give = second_conv(jnp.stack(ids).astype(jnp.int32), w2, k2, near + far)

    got = lax.ppermute(give, "core", shift("core", 1))
    both = (keep.astype(jnp.float32) + got.astype(jnp.float32)).astype(jnp.bfloat16)
    terms = lax.all_to_all(both.reshape(8, 96, 512), ("xh", "y"), 0, 0, tiled=True)
    total = jnp.sum(terms.astype(jnp.float32), axis=0).T
    return (inputs.astype(jnp.float32) + total.reshape(inputs.shape)).astype(jnp.bfloat16)


def solution(mesh):
    fine = Mesh(mesh.devices.reshape(2, 8, 2, 2, 4), AXES)
    row_slab, col = ("xl", "z", "y"), ("xh", "core")
    return jax.shard_map(
        layer,
        mesh=fine,
        in_specs=(P(col, None, row_slab), P(None, None, row_slab, col), P(None, None, col, row_slab)),
        out_specs=P(col, None, row_slab),
        check_vma=False,
    )
```
